768 devices in a mesh: batch: 8 (over x, core), ctx: 48 (over z, y_hi), head: 2 (over y_lo).
Axes of the slice: x: 4, y: 8 (y_hi: 4, y_lo: 2; y = y_hi * 2 + y_lo), z: 12, core: 2. Of those that a mesh axis runs over, the one named last changes fastest.
Arguments:
- queries: bfloat16 [2, 49152, 1536], P(None, ('batch', 'ctx'), 'head'), parts along dimension 1, may hold values from -6 to 6
- keyvals: bfloat16 [4, 49152, 1536], P(None, ('batch', 'ctx'), 'head'), parts along dimension 1, may hold values from -6 to 6
- w_out: bfloat16 [1536, 3072], P('head'), may hold values from -2.390625 to 2.390625
Outputs:
- output: bfloat16 [49152, 3072], P(('batch', 'ctx'), 'head'), parts along dimension 0
- output_tangent: bfloat16 [49152, 3072], P(('batch', 'ctx'), 'head'), parts along dimension 0
The draws below stay inside these ranges and needn't reach their ends.
There are 8 independent parts, one for each index of `batch`. The reference program is written for one: setup_inputs(seed, part) draws one part's arguments, and reference() takes and returns one part's arrays. A program takes and returns all parts, laid end to end along the dimension named above; an argument that names none is the same for every part. Nothing has to cross between parts.
All inputs are finite; a program needn't handle non-finite values.
Results may differ from the reference program's by a relative error of at most 0.01.
Values may be sent and summed in bfloat16 or wider, within the bound.
No kernel may reach another device: no remote copies, remote signals or barrier semaphores. Data moves between devices by JAX's collectives and lax.ppermute only.
A program may use at most 32 MiB of HBM per device.

```python
import math
import jax
import jax.numpy as jnp
from jax import lax

D = 3072
HEADS = 12
HD = 128
RADIUS = 2
TOK_DEV = 128
SEQ = 6144
N_CTX = 48


def base_values(key, shape):
    return jnp.clip(jax.random.normal(key, shape, jnp.float32), -6.0, 6.0)


def draw_queries(key, part):
    values = base_values(jax.random.fold_in(key, 1), (2, SEQ, HEADS * HD))
    return values.astype(jnp.bfloat16)


def draw_keyvals(key, part):
    values = base_values(jax.random.fold_in(key, 2), (4, SEQ, HEADS * HD))
    return values.astype(jnp.bfloat16)


def levels(stream_key, dims, cuts, least, top_value):
    def one(dim, parts):
        heights = jax.random.uniform(jax.random.fold_in(jax.random.fold_in(stream_key, 6), dim), (parts,), jnp.float32, least / len(cuts), top_value / len(cuts))
        return jnp.repeat(jnp.exp(heights), dims[dim] // parts).reshape((-1,) + (1,) * (len(dims) - dim - 1))

    factor_of = one(*cuts[0])
    for cut in cuts[1:]:
        factor_of = factor_of * one(*cut)
    return factor_of


def noise(key, shape, deviation, reach, cuts=(), held_as=jnp.bfloat16):
    entries = deviation * jax.random.normal(key, shape, jnp.float32)
    if cuts:
        entries = entries * levels(key, shape, cuts, -0.22, 0.18)
    return jnp.clip(entries, -reach, reach).astype(held_as)


def setup_inputs(seed: int = 0, part: int = 0) -> dict:
    key_of = jax.random.split(jax.random.key(seed), 4)
    own_keys = jax.random.split(jax.random.fold_in(key_of[3], part), 4)
    return {
        "queries": draw_queries(jax.random.fold_in(jax.random.fold_in(key_of[3], part), 71), part),
        "keyvals": draw_keyvals(jax.random.fold_in(jax.random.fold_in(key_of[3], part), 71), part),
        "w_out": noise(key_of[2], (HEADS * HD, D), 0.4, 2.390625, ((0, 2),)),
    }


def attend(query_pair, key_block, visible, w_out):
    row_count = query_pair.shape[1]
    key_count = key_block.shape[1]
    head_count = query_pair.shape[2] // HD
    score_scale = 1.0 / math.sqrt(HD)
    query_now = query_pair[0].reshape(row_count, head_count, HD).astype(jnp.float32)
    query_tan = query_pair[1].reshape(row_count, head_count, HD).astype(jnp.float32)
    key_now = key_block[0].reshape(key_count, head_count, HD).astype(jnp.float32)
    value_now = key_block[1].reshape(key_count, head_count, HD).astype(jnp.float32)
    key_tan = key_block[2].reshape(key_count, head_count, HD).astype(jnp.float32)
    value_tan = key_block[3].reshape(key_count, head_count, HD).astype(jnp.float32)
    scores = jnp.einsum('qhd,khd->hqk', query_now, key_now) * score_scale
    scores = jnp.where(visible[None, None, :], scores, -jnp.inf)
    row_max = lax.optimization_barrier(jnp.max(scores, axis=-1, keepdims=True))
    expo = jnp.exp(scores - row_max)
    prob_f = expo / lax.optimization_barrier(jnp.sum(expo, axis=-1, keepdims=True))
    tan_scores = (jnp.einsum('qhd,khd->hqk', query_tan, key_now) + jnp.einsum('qhd,khd->hqk', query_now, key_tan)) * score_scale
    weighted = prob_f * tan_scores
    tan_shift = lax.optimization_barrier(jnp.sum(weighted, axis=-1))
    prob_b = prob_f.astype(jnp.bfloat16).astype(jnp.float32)
    weight_b = weighted.astype(jnp.bfloat16).astype(jnp.float32)
    attended = jnp.einsum('hqk,khd->qhd', prob_b, value_now)
    att_tan = jnp.einsum('hqk,khd->qhd', weight_b, value_now) + jnp.einsum('hqk,khd->qhd', prob_b, value_tan) - jnp.transpose(tan_shift)[:, :, None] * attended
    att_flat = attended.reshape(row_count, head_count * HD).astype(jnp.bfloat16)
    tan_flat = att_tan.reshape(row_count, head_count * HD).astype(jnp.bfloat16)
    projected = jnp.dot(att_flat, w_out, preferred_element_type=jnp.float32)
    projected_tan = jnp.dot(tan_flat, w_out, preferred_element_type=jnp.float32)
    return (projected, projected_tan)

def reference(queries, keyvals, w_out):
    margin = RADIUS * TOK_DEV
    padded = jnp.pad(keyvals, ((0, 0), (margin, margin), (0, 0)))
    key_count = (2 * RADIUS + 1) * TOK_DEV
    offsets = jnp.arange(key_count, dtype=jnp.int32) // TOK_DEV - RADIUS

    def one_block(block):
        start = (block * TOK_DEV).astype(jnp.int32)
        query_pair = lax.dynamic_slice_in_dim(queries, start, TOK_DEV, 1)
        key_block = lax.dynamic_slice_in_dim(padded, start, key_count, 1)
        target = block + offsets
        visible = (target >= 0) & (target < N_CTX)
        return attend(query_pair, key_block, visible, w_out)
    projected, projected_tan = lax.map(one_block, jnp.arange(N_CTX, dtype=jnp.int32))
    output = projected.reshape(N_CTX * TOK_DEV, D).astype(jnp.bfloat16)
    output_tangent = projected_tan.reshape(N_CTX * TOK_DEV, D).astype(jnp.bfloat16)
    return (output, output_tangent)
```

```python
import functools
import math

import jax
import jax.numpy as jnp
from jax import lax
from jax.experimental import pallas as pl
from jax.experimental.pallas import tpu as pltpu
from jax.sharding import PartitionSpec as P

HD = 128
TOK = 128
ROW = 4
WIN = 5 * TOK
SCALE = 1.0 / math.sqrt(HD)
NT = (((1,), (1,)), ((), ()))


def prep_kernel(info, kv, q, send, q_send, q_own):
    for d in range(ROW):
        for t in range(4):
            send[d, t] = kv[t, :, d * HD : (d + 1) * HD]
            s = 4 + d % 2
            send[d, 4 + t] = kv[t, :, s * HD : (s + 1) * HD]
        for t in range(2):
            send[d, 8 + t] = q[t, :, d * HD : (d + 1) * HD]
    odd = info[0] % 2

    @pl.when(odd == 0)
    def _():
        q_own[...] = q[:, :, 4 * HD : 5 * HD]
        q_send[...] = q[:, :, 5 * HD : 6 * HD]

    @pl.when(odd == 1)
    def _():
        q_own[...] = q[:, :, 5 * HD : 6 * HD]
        q_send[...] = q[:, :, 4 * HD : 5 * HD]


def unit(qn, qt, k, v, kt, vt, first_tile, tiles):
    s = lax.dot_general(qn, k, NT, preferred_element_type=jnp.float32) * SCALE
    tile = first_tile + lax.broadcasted_iota(jnp.int32, (1, WIN), 1) // TOK
    s = jnp.where((tile >= 0) & (tile < tiles), s, -jnp.inf)
    e = jnp.exp(s - jnp.max(s, axis=-1, keepdims=True))
    p = e * (1.0 / jnp.sum(e, axis=-1, keepdims=True))
    t = SCALE * lax.dot_general(
        jnp.concatenate([qt, qn], axis=1),
        jnp.concatenate([k, kt], axis=1),
        NT,
        preferred_element_type=jnp.float32,
    )
    w = p * t
    shift = jnp.sum(w, axis=-1, keepdims=True)
    pb = p.astype(jnp.bfloat16)
    wb = w.astype(jnp.bfloat16)
    att = jnp.dot(pb, v, preferred_element_type=jnp.float32)
    tan = (
        jnp.dot(wb, v, preferred_element_type=jnp.float32)
        + jnp.dot(pb, vt, preferred_element_type=jnp.float32)
        - shift * att
    )
    return att.astype(jnp.bfloat16), tan.astype(jnp.bfloat16)


def attend_kernel(tiles, info, r, ha, hb, q_own, q_recv, o_full, o_own, o_other, kf, ks):
    place = info[0]
    q = place % ROW
    row_start = place - q
    odd = q % 2
    low = q < 2
    for t in range(4):
        for j in range(ROW):
            kf[t, (2 + j) * TOK : (3 + j) * TOK, :] = r[j, t]

    @pl.when(low)
    def _():
        for t in range(4):
            for j in range(2):
                kf[t, j * TOK : (j + 1) * TOK, :] = ha[j, t]
                kf[t, (6 + j) * TOK : (7 + j) * TOK, :] = hb[j, t]
                ks[t, j * TOK : (j + 1) * TOK, :] = ha[j, 4 + t]
            for j in range(ROW):
                ks[t, (2 + j) * TOK : (3 + j) * TOK, :] = r[j, 4 + t]

    @pl.when(jnp.logical_not(low))
    def _():
        for t in range(4):
            for j in range(2):
                kf[t, j * TOK : (j + 1) * TOK, :] = hb[j, t]
                kf[t, (6 + j) * TOK : (7 + j) * TOK, :] = ha[j, t]
                ks[t, (4 + j) * TOK : (5 + j) * TOK, :] = ha[j, 4 + t]
            for j in range(ROW):
                ks[t, j * TOK : (j + 1) * TOK, :] = r[j, 4 + t]

    for j in range(ROW):
        at = slice(j * TOK, j * TOK + WIN)
        a, b = unit(
            r[j, 8], r[j, 9], kf[0, at, :], kf[1, at, :], kf[2, at, :], kf[3, at, :],
            row_start + j - 2, tiles,
        )
        o_full[j, 0] = a
        o_full[j, 1] = b
    base = row_start + jnp.where(low, -2, 0)
    for u, qq, out in ((odd, q_own, o_own), (1 - odd, q_recv, o_other)):
        at = pl.ds(pl.multiple_of(u * TOK, TOK), WIN)
        a, b = unit(
            qq[0], qq[1], ks[0, at, :], ks[1, at, :], ks[2, at, :], ks[3, at, :],
            base + u, tiles,
        )
        out[0] = a
        out[1] = b


def far_kernel(info, g, own, recv, w, part, lhs, a):
    @pl.when(pl.program_id(0) == 0)
    def _():
        odd = info[0] % 2
        for t in range(2):
            for h in range(4):
                a[t * TOK : (t + 1) * TOK, h * HD : (h + 1) * HD] = g[h, t]

        @pl.when(odd == 0)
        def _():
            for t in range(2):
                a[t * TOK : (t + 1) * TOK, 4 * HD : 5 * HD] = own[t]
                a[t * TOK : (t + 1) * TOK, 5 * HD : 6 * HD] = recv[t]

        @pl.when(odd == 1)
        def _():
            for t in range(2):
                a[t * TOK : (t + 1) * TOK, 4 * HD : 5 * HD] = recv[t]
                a[t * TOK : (t + 1) * TOK, 5 * HD : 6 * HD] = own[t]

        lhs[...] = a[...]

    part[...] = jnp.dot(a[...], w[...], preferred_element_type=jnp.float32).astype(part.dtype)


def near_kernel(info, lhs, w, part):
    part[...] = jnp.dot(lhs[...], w[...], preferred_element_type=jnp.float32)


def vmem():
    return pl.BlockSpec(memory_space=pltpu.VMEM)


def per_device(queries, keyvals, w_out):
    bf16 = jnp.bfloat16
    ctx_count = lax.axis_size("ctx")
    rows = ctx_count // ROW
    place = lax.axis_index("ctx").astype(jnp.int32)
    side = lax.axis_index("head").astype(jnp.int32)
    info = jnp.stack([place, side])
    low = place % ROW < 2
    smem = pl.BlockSpec(memory_space=pltpu.SMEM)

    send, q_send, q_own = pl.pallas_call(
        prep_kernel,
        in_specs=[smem, vmem(), vmem()],
        out_specs=[vmem()] * 3,
        out_shape=[
            jax.ShapeDtypeStruct((ROW, 10, TOK, HD), bf16),
            jax.ShapeDtypeStruct((2, TOK, HD), bf16),
            jax.ShapeDtypeStruct((2, TOK, HD), bf16),
        ],
        name="prep",
    )(info, keyvals, queries)

    swap = [(i, i ^ 1) for i in range(ctx_count)]
    q_recv = lax.ppermute(q_send, "ctx", swap)
    groups = [[z * ROW + j for j in range(ROW)] for z in range(rows)]
    r = lax.all_to_all(send, "ctx", 0, 0, axis_index_groups=groups, tiled=True)

    up = {i: i + ROW for i in range(ctx_count - ROW)}
    down = {i: i - ROW for i in range(ROW, ctx_count)}
    near_pairs = [(i, d) for i, d in up.items() if i % ROW < 2]
    near_pairs += [(i, d) for i, d in down.items() if i % ROW >= 2]
    far_pairs = [(i, d) for i, d in down.items() if i % ROW < 2]
    far_pairs += [(i, d) for i, d in up.items() if i % ROW >= 2]
    zero = jnp.int32(0)
    two = jnp.int32(2)
    ha = lax.dynamic_slice(r, (jnp.where(low, two, zero), zero, zero, zero), (2, 8, TOK, HD))
    hb = lax.dynamic_slice(r, (jnp.where(low, zero, two), zero, zero, zero), (2, 4, TOK, HD))
    ha = lax.ppermute(ha, "ctx", near_pairs)
    hb = lax.ppermute(hb, "ctx", far_pairs)

    o_full, o_own, o_other = pl.pallas_call(
        functools.partial(attend_kernel, ctx_count),
        in_specs=[smem] + [vmem()] * 5,
        out_specs=[vmem()] * 3,
        out_shape=[
            jax.ShapeDtypeStruct((ROW, 2, TOK, HD), bf16),
            jax.ShapeDtypeStruct((2, TOK, HD), bf16),
            jax.ShapeDtypeStruct((2, TOK, HD), bf16),
        ],
        scratch_shapes=[
            pltpu.VMEM((4, 8 * TOK, HD), bf16),
            pltpu.VMEM((4, 6 * TOK, HD), bf16),
        ],
        cost_estimate=pl.CostEstimate(flops=800_000_000, bytes_accessed=3_000_000, transcendentals=500_000),
        name="attend",
    )(info, r, ha, hb, q_own, q_recv)

    o_recv = lax.ppermute(o_other, "ctx", swap)
    g = lax.all_to_all(o_full, "ctx", 0, 0, axis_index_groups=groups, tiled=True)

    depth, width = w_out.shape
    half = width // 2
    block = half // 3
    far, lhs = pl.pallas_call(
        far_kernel,
        grid_spec=pltpu.PrefetchScalarGridSpec(
            num_scalar_prefetch=1,
            grid=(3,),
            in_specs=[
                pl.BlockSpec((4, 2, TOK, HD), lambda j, s: (0, 0, 0, 0)),
                pl.BlockSpec((2, TOK, HD), lambda j, s: (0, 0, 0)),
                pl.BlockSpec((2, TOK, HD), lambda j, s: (0, 0, 0)),
                pl.BlockSpec((depth, block), lambda j, s: (0, (1 - s[1]) * 3 + j)),
            ],
            out_specs=[
                pl.BlockSpec((2 * TOK, block), lambda j, s: (0, j)),
                pl.BlockSpec((2 * TOK, depth), lambda j, s: (0, 0)),
            ],
            scratch_shapes=[pltpu.VMEM((2 * TOK, depth), bf16)],
        ),
        out_shape=[
            jax.ShapeDtypeStruct((2 * TOK, half), bf16),
            jax.ShapeDtypeStruct((2 * TOK, depth), bf16),
        ],
        cost_estimate=pl.CostEstimate(flops=600_000_000, bytes_accessed=4_000_000, transcendentals=0),
        name="far",
    )(info, g, o_own, o_recv, w_out)
    far = lax.ppermute(far, "head", [(0, 1), (1, 0)])
    near = pl.pallas_call(
        near_kernel,
        grid_spec=pltpu.PrefetchScalarGridSpec(
            num_scalar_prefetch=1,
            grid=(3,),
            in_specs=[
                pl.BlockSpec((2 * TOK, depth), lambda j, s: (0, 0)),
                pl.BlockSpec((depth, block), lambda j, s: (0, s[1] * 3 + j)),
            ],
            out_specs=pl.BlockSpec((2 * TOK, block), lambda j, s: (0, j)),
        ),
        out_shape=jax.ShapeDtypeStruct((2 * TOK, half), jnp.float32),
        cost_estimate=pl.CostEstimate(flops=600_000_000, bytes_accessed=4_000_000, transcendentals=0),
        name="near",
    )(info, lhs, w_out)
    total = (near + far.astype(jnp.float32)).astype(bf16)
    return (total[:TOK], total[TOK:])


def solution(mesh):
    in_specs = (
        P(None, ("batch", "ctx"), "head"),
        P(None, ("batch", "ctx"), "head"),
        P("head", None),
    )
    out_specs = (P(("batch", "ctx"), "head"), P(("batch", "ctx"), "head"))
    return jax.shard_map(
        per_device, mesh=mesh, in_specs=in_specs, out_specs=out_specs, check_vma=False
    )
```
